32 devices in a mesh: ex: 4 (over z), ft: 8 (over y, x, core).
Axes of the slice: x: 2, y: 2, z: 4, core: 2. Of those that a mesh axis runs over, the one named last changes fastest.
Arguments:
- tiles: bfloat16 [3072, 128, 128], P(('ex', 'ft')), may hold values from -0.5 to 0.5
- tile_count: int32 [32], P(('ex', 'ft')), may hold values from 16 to 96, as said below
- tile_cslot: int32 [3072], P(('ex', 'ft')), may hold values from 0 to 31
- tile_rslot: int32 [3072], P(('ex', 'ft')), may hold values from 0 to 31
- need_cols: int32 [32, 4, 8], P(('ex', 'ft')), may hold values from 0 to 127
- fold_rows: int32 [32, 8, 4], P(('ex', 'ft')), may hold values from 0 to 7
- weights: float32 [64, 4, 128], P('ft', 'ex'), may hold values from 0.01 to 0.25
- directions: float32 [512, 8, 2, 128], P('ex', 'ft'), may hold values from -6 to 6
Outputs:
- hessvec: float32 [512, 8, 2, 128], P('ex', 'ft')
The draws below stay inside these ranges and needn't reach their ends.
Inputs may be any that keep to these rules, and one draw needn't show every extreme that they name: tile_count reaches 96 on some device in every draw; the mean is about a third of that.
All inputs are finite; a program needn't handle non-finite values.
Results may differ from the reference program's by a relative error of at most 0.0024.
Values may be sent and summed in bfloat16 or wider, within the bound.
A program may use at most 64 MiB of HBM per device.

```python
import math
import jax
import jax.numpy as jnp
from jax import lax

TILE_SIDE = 128
TILE_SLOTS = 96
COL_BLOCKS = 128
ROW_BLOCKS = 8
COL_ASKS = 8
ROW_SLOTS = 4
NUM_VECS = 2
GROUP_COLS = 512
GROUP_ROWS = 64
N_EX = 4
N_FT = 8
DEVICES = 32


def draw_tile_count(key, part):
    first_key = jax.random.fold_in(key, 11)
    second_key = jax.random.fold_in(key, 23)
    counts = jax.random.randint(first_key, (DEVICES,), TILE_SLOTS // 6, TILE_SLOTS // 2 + 1, dtype=jnp.int32)
    order = jax.random.permutation(second_key, DEVICES)
    return counts.at[order[0]].set(TILE_SLOTS).astype(jnp.int32)


def set_ends(entries, own_key, smallest, high):
    index_at = [jax.random.randint(jax.random.fold_in(own_key, axis), (), 0, length) for axis, length in enumerate(entries.shape)]
    longest = entries.shape.index(max(entries.shape))
    next_to = index_at[:longest] + [(index_at[longest] + 1) % entries.shape[longest]] + index_at[longest + 1:]
    return entries.at[tuple(index_at)].set(smallest).at[tuple(next_to)].set(high)


def block_scale(own_key, extent, pieces, low, high):
    loudness = 1.0
    for position, shards_of in pieces:
        steps = jax.random.uniform(jax.random.fold_in(jax.random.fold_in(own_key, 6), position), (shards_of,), jnp.float32, low / len(pieces), high / len(pieces))
        loudness = loudness * jnp.repeat(jnp.exp(steps), extent[position] // shards_of).reshape((-1,) + (1,) * (len(extent) - 1 - position))
    return loudness


def gaussian(stream_key, dims, width, reach, shards=(), kind=jnp.bfloat16):
    loudness = block_scale(stream_key, dims, shards, -0.22, 0.18) if shards else 1.0
    drawn = jax.random.normal(stream_key, dims, jnp.float32) * width * loudness
    return jnp.minimum(jnp.maximum(drawn, -reach), reach).astype(kind)


def setup_inputs(seed: int = 0) -> dict:
    seeds = jax.random.split(jax.random.key(seed), 9)
    return {
        "tiles": gaussian(seeds[0], (DEVICES * TILE_SLOTS, TILE_SIDE, TILE_SIDE), TILE_SIDE ** -0.5, 0.5, ((0, 32),)),
        "tile_count": draw_tile_count(jax.random.fold_in(seeds[8], 71), 0),
        "tile_cslot": set_ends(jax.random.randint(seeds[2], (DEVICES * TILE_SLOTS,), 0, N_EX * COL_ASKS), jax.random.fold_in(seeds[2], 1), 0, (N_EX * COL_ASKS) - 1).astype(jnp.int32),
        "tile_rslot": set_ends(jax.random.randint(seeds[3], (DEVICES * TILE_SLOTS,), 0, N_FT * ROW_SLOTS), jax.random.fold_in(seeds[3], 1), 0, (N_FT * ROW_SLOTS) - 1).astype(jnp.int32),
        "need_cols": set_ends(jax.random.randint(seeds[4], (DEVICES, N_EX, COL_ASKS), 0, COL_BLOCKS), jax.random.fold_in(seeds[4], 1), 0, COL_BLOCKS - 1).astype(jnp.int32),
        "fold_rows": set_ends(jax.random.randint(seeds[5], (DEVICES, N_FT, ROW_SLOTS), 0, ROW_BLOCKS), jax.random.fold_in(seeds[5], 1), 0, ROW_BLOCKS - 1).astype(jnp.int32),
        "weights": jnp.clip(jnp.exp(math.log(0.25) - 3.218876 * jax.random.uniform(seeds[6], (GROUP_ROWS, N_EX, TILE_SIDE), jnp.float32) ** block_scale(seeds[6], (GROUP_ROWS, N_EX, TILE_SIDE), ((0, 8), (1, 4)), -0.2, 0.2)), 0.01, 0.25),
        "directions": gaussian(seeds[7], (GROUP_COLS, N_FT, NUM_VECS, TILE_SIDE), 1.0, 6.0, ((0, 4), (1, 8)), jnp.float32),
    }


def reference(tiles, tile_count, tile_cslot, tile_rslot, need_cols, fold_rows, weights, directions):
    vec_flat = directions.transpose(1, 0, 2, 3).reshape(N_FT * GROUP_COLS, NUM_VECS, TILE_SIDE)
    vec_bf = lax.optimization_barrier(vec_flat.astype(jnp.bfloat16))
    weight_flat = weights.transpose(1, 0, 2).reshape(N_EX * GROUP_ROWS, TILE_SIDE)
    tiles_dev = tiles.reshape(DEVICES, TILE_SLOTS, TILE_SIDE, TILE_SIDE)
    cslots = tile_cslot.reshape(DEVICES, TILE_SLOTS)
    rslots = tile_rslot.reshape(DEVICES, TILE_SLOTS)
    owner_cols = jnp.arange(N_EX, dtype=jnp.int32)[:, None] * COL_BLOCKS
    owner_rows = jnp.arange(N_FT, dtype=jnp.int32)[:, None] * ROW_BLOCKS
    slot_range = jnp.arange(TILE_SLOTS, dtype=jnp.int32)
    devices_ids = jnp.arange(DEVICES, dtype=jnp.int32)

    def places(device_id, col_list, row_list, cslot, rslot):
        ex_index = device_id // N_FT
        ft_index = device_id % N_FT
        col_map = (owner_cols + col_list).reshape(-1)
        row_map = (owner_rows + row_list).reshape(-1)
        global_cols = (ft_index * GROUP_COLS + col_map[cslot]).astype(jnp.int32)
        global_rows = (ex_index * GROUP_ROWS + row_map[rslot]).astype(jnp.int32)
        return global_cols, global_rows

    items = (devices_ids, tiles_dev, cslots, rslots, need_cols, fold_rows, tile_count)

    def forward(running, device_item):
        device_id, tile_set, cslot, rslot, col_list, row_list, live_count = device_item
        global_cols, global_rows = places(device_id, col_list, row_list, cslot, rslot)
        live_mask = slot_range < live_count
        inputs = vec_bf[global_cols].astype(jnp.float32)
        result = jnp.einsum('tij,tkj->tki', tile_set.astype(jnp.float32), inputs)
        result = jnp.where(live_mask[:, None, None], result, jnp.zeros_like(result))
        return running.at[global_rows].add(result), None

    margins, _ = lax.scan(forward, jnp.zeros((N_EX * GROUP_ROWS, NUM_VECS, TILE_SIDE), jnp.float32), items)
    scaled = lax.optimization_barrier((weight_flat[:, None, :] * margins).astype(jnp.bfloat16))

    def backward(running, device_item):
        device_id, tile_set, cslot, rslot, col_list, row_list, live_count = device_item
        global_cols, global_rows = places(device_id, col_list, row_list, cslot, rslot)
        live_mask = slot_range < live_count
        inputs = scaled[global_rows].astype(jnp.float32)
        result = jnp.einsum('tij,tki->tkj', tile_set.astype(jnp.float32), inputs)
        result = jnp.where(live_mask[:, None, None], result, jnp.zeros_like(result))
        return running.at[global_cols].add(result), None

    curvature, _ = lax.scan(backward, jnp.zeros((N_FT * GROUP_COLS, NUM_VECS, TILE_SIDE), jnp.float32), items)
    hess_flat = vec_flat + 4.0 * curvature
    return hess_flat.reshape(N_FT, GROUP_COLS, NUM_VECS, TILE_SIDE).transpose(1, 0, 2, 3)
```

```python
import functools
import jax
import jax.numpy as jnp
from jax import lax
from jax.experimental import pallas as pl
from jax.experimental.pallas import tpu as pltpu
from jax.sharding import PartitionSpec as P

scale_back = 4.0
tile_batch = 8


def exchange(axis, n, me, out_ref, in_ref, send_sem, recv_sem):
    copies = []
    for d in range(1, n):
        copy = pltpu.make_async_remote_copy(
            src_ref=out_ref.at[lax.rem(me + d, n)],
            dst_ref=in_ref.at[me],
            send_sem=send_sem.at[d],
            recv_sem=recv_sem.at[d],
            device_id={axis: lax.rem(me + d, n)},
            device_id_type=pl.DeviceIdType.MESH,
        )
        copy.start()
        copies.append(copy)
    return copies


def split_three(x):
    high = x.astype(jnp.bfloat16)
    rest = x - high.astype(jnp.float32)
    middle = rest.astype(jnp.bfloat16)
    low = (rest - middle.astype(jnp.float32)).astype(jnp.bfloat16)
    return jnp.concatenate([high, middle, low], axis=0)


def kernel(
    n_ex, n_ft, num_vecs,
    count_ref, cslot_ref, rslot_ref, need_ref, fold_ref, weight_ref, tiles_hbm, dir_hbm,
    out_ref,
    tiles_v, dir_v, need_out, need_in, fold_out, fold_in, vec_out, vec_in,
    mar_out, mar_in, sc_out, sc_in, cur_out, cur_in,
    col_f, row_f, spread, collect, place, local_sem, *sems,
):
    f32, bf16, i32 = jnp.float32, jnp.bfloat16, jnp.int32
    ex_me, ft_me = lax.axis_index("ex"), lax.axis_index("ft")
    asks, slots = need_ref.shape[2], fold_ref.shape[2]
    row_blocks = weight_ref.shape[0]
    slot_count, side = tiles_v.shape[0], tiles_v.shape[1]
    ask_rows, slot_rows = num_vecs * asks, num_vecs * slots
    all_asks, all_slots = n_ex * ask_rows, n_ft * slot_rows

    dir_copy = pltpu.make_async_copy(dir_hbm, dir_v, local_sem.at[0])
    dir_copy.start()
    tile_copy = pltpu.make_async_copy(tiles_hbm, tiles_v, local_sem.at[1])
    tile_copy.start()

    barrier = pltpu.get_barrier_semaphore()
    for d in range(1, n_ex):
        pl.semaphore_signal(barrier, inc=1, device_id={"ex": lax.rem(ex_me + d, n_ex)},
                            device_id_type=pl.DeviceIdType.MESH)
    for d in range(1, n_ft):
        pl.semaphore_signal(barrier, inc=1, device_id={"ft": lax.rem(ft_me + d, n_ft)},
                            device_id_type=pl.DeviceIdType.MESH)

    sub = lax.broadcasted_iota(i32, (asks, side), 0)
    for o in range(n_ex):
        block = jnp.zeros((asks, side), i32)
        for j in range(asks):
            block = jnp.where(sub == j, need_ref[0, o, j], block)
        need_out[o] = block
    sub = lax.broadcasted_iota(i32, (slot_rows, side), 0)
    for q in range(n_ft):
        block = jnp.zeros((slot_rows, side), i32)
        for i in range(slots):
            block = jnp.where(sub % slots == i, fold_ref[0, q, i], block)
        fold_out[q] = block + (sub // slots) * row_blocks

    pl.semaphore_wait(barrier, n_ex - 1 + n_ft - 1)

    need_copies = exchange("ex", n_ex, ex_me, need_out, need_in, sems[0], sems[1])
    fold_copies = exchange("ft", n_ft, ft_me, fold_out, fold_in, sems[2], sems[3])
    need_in[ex_me] = need_out[ex_me]
    fold_in[ft_me] = fold_out[ft_me]

    dir_copy.wait()
    dir_bf = dir_v[...].astype(bf16)
    col_rows = dir_v.shape[0]
    for copy in need_copies:
        copy.wait()
    asked = need_in[...]
    asked = jnp.concatenate([asked * num_vecs + k for k in range(num_vecs)], axis=1)
    asked = asked.reshape(all_asks, side)
    lane = lax.broadcasted_iota(i32, (all_asks, side), 1)
    hot = jnp.concatenate(
        [jnp.where(lane + base == asked, 1.0, 0.0) for base in range(0, col_rows, side)], axis=1
    )
    picked = jnp.dot(hot.astype(bf16), dir_bf, preferred_element_type=f32)
    vec_out[...] = picked.astype(bf16).reshape(vec_out.shape)
    vec_copies = exchange("ex", n_ex, ex_me, vec_out, vec_in, sems[4], sems[5])
    vec_in[ex_me] = vec_out[ex_me]

    spread[...] = hot.T.astype(bf16)
    for copy in fold_copies:
        copy.wait()
    lane = lax.broadcasted_iota(i32, (all_slots, side), 1)
    rows_hot = jnp.where(fold_in[...].reshape(all_slots, side) == lane, 1.0, 0.0)
    place[...] = rows_hot.astype(bf16)
    collect[...] = rows_hot.T[: num_vecs * row_blocks].astype(bf16)
    weight = jnp.concatenate([weight_ref[...]] * num_vecs, axis=0)

    for copy in vec_copies:
        copy.wait()
    col_f[...] = vec_in[...].reshape(all_asks, side).astype(f32)
    tile_copy.wait()

    live = count_ref[0]
    row_id = lax.broadcasted_iota(i32, (all_slots, side), 0)
    row_slot = (row_id // slot_rows) * slots + row_id % slots
    half = lax.broadcasted_iota(i32, (slot_rows, side), 0) // slots

    def forward(step, total):
        lefts, rights = [], []
        for u in range(tile_batch):
            t = step * tile_batch + u
            c, r = cslot_ref[t], rslot_ref[t]
            r = jnp.where(t < live, r, -1)
            base = (c // asks) * ask_rows + c % asks
            value = jnp.broadcast_to(col_f[pl.ds(base, 1), :], (slot_rows, side))
            for k in range(1, num_vecs):
                other = jnp.broadcast_to(col_f[pl.ds(base + k * asks, 1), :], (slot_rows, side))
                value = jnp.where(half >= k, other, value)
            value = jnp.concatenate([value] * n_ft, axis=0)
            lefts.append(jnp.where(row_slot == r, value, 0.0).astype(bf16))
            rights.append(tiles_v[t])
        return total + lax.dot_general(
            jnp.concatenate(lefts, axis=1), jnp.concatenate(rights, axis=1),
            (((1,), (1,)), ((), ())), preferred_element_type=f32,
        )

    part = lax.fori_loop(0, slot_count // tile_batch, forward, jnp.zeros((all_slots, side), f32))
    mar_out[...] = part.reshape(mar_out.shape)
    mar_copies = exchange("ft", n_ft, ft_me, mar_out, mar_in, sems[6], sems[7])
    mar_in[ft_me] = mar_out[ft_me]
    for copy in mar_copies:
        copy.wait()
    pieces = split_three(mar_in[...].reshape(all_slots, side))
    gather = collect[...]
    margins = jnp.dot(
        jnp.concatenate([gather] * 3, axis=1), pieces, preferred_element_type=f32
    )
    scaled = weight * margins
    filler = jnp.zeros((side - num_vecs * row_blocks, side), f32)
    scaled = jnp.concatenate([scaled, filler], axis=0).astype(bf16)
    answer = jnp.dot(place[...], scaled, preferred_element_type=f32)
    sc_out[...] = answer.astype(sc_out.dtype).reshape(sc_out.shape)
    sc_copies = exchange("ft", n_ft, ft_me, sc_out, sc_in, sems[8], sems[9])
    sc_in[ft_me] = sc_out[ft_me]
    for copy in sc_copies:
        copy.wait()
    row_f[...] = sc_in[...].astype(f32).reshape(all_slots, side)

    col_id = lax.broadcasted_iota(i32, (all_asks, side), 0)
    col_slot = (col_id // ask_rows) * asks + col_id % asks

    def backward(step, total):
        lefts, rights = [], []
        for u in range(tile_batch):
            t = step * tile_batch + u
            c, r = cslot_ref[t], rslot_ref[t]
            c = jnp.where(t < live, c, -1)
            base = (r // slots) * slot_rows + r % slots
            values = [
                jnp.broadcast_to(row_f[pl.ds(base + k * slots, 1), :], (asks, side))
                for k in range(num_vecs)
            ]
            value = jnp.concatenate(values * n_ex, axis=0)
            lefts.append(jnp.where(col_slot == c, value, 0.0).astype(bf16))
            rights.append(tiles_v[t])
        return total + jnp.dot(
            jnp.concatenate(lefts, axis=1), jnp.concatenate(rights, axis=0),
            preferred_element_type=f32,
        )

    part = lax.fori_loop(0, slot_count // tile_batch, backward, jnp.zeros((all_asks, side), f32))
    cur_out[...] = part.reshape(cur_out.shape)
    cur_copies = exchange("ex", n_ex, ex_me, cur_out, cur_in, sems[10], sems[11])
    cur_in[ex_me] = cur_out[ex_me]
    for copy in cur_copies:
        copy.wait()
    pieces = split_three(cur_in[...].reshape(all_asks, side))
    scatter = spread[...]
    curvature = jnp.dot(
        jnp.concatenate([scatter] * 3, axis=1), pieces, preferred_element_type=f32
    )
    out_ref[...] = dir_v[...] + scale_back * curvature


def local(tiles, tile_count, tile_cslot, tile_rslot, need_cols, fold_rows, weights, directions):
    n_ex, n_ft = lax.axis_size("ex"), lax.axis_size("ft")
    side = tiles.shape[1]
    col_blocks, num_vecs = directions.shape[0], directions.shape[2]
    row_blocks = weights.shape[0]
    asks, slots = need_cols.shape[2], fold_rows.shape[2]
    ask_rows, slot_rows = num_vecs * asks, num_vecs * slots
    f32, bf16, i32 = jnp.float32, jnp.bfloat16, jnp.int32
    smem = pl.BlockSpec(memory_space=pltpu.SMEM)
    vmem = pl.BlockSpec(memory_space=pltpu.VMEM)
    hbm = pl.BlockSpec(memory_space=pl.ANY)
    pairs = [n_ex, n_ft, n_ex, n_ft, n_ft, n_ex]
    out = pl.pallas_call(
        functools.partial(kernel, n_ex, n_ft, num_vecs),
        out_shape=jax.ShapeDtypeStruct((col_blocks * num_vecs, side), f32),
        in_specs=[smem] * 5 + [vmem, hbm, hbm],
        out_specs=vmem,
        scratch_shapes=[
            pltpu.VMEM(tiles.shape, bf16),
            pltpu.VMEM((col_blocks * num_vecs, side), f32),
            pltpu.VMEM((n_ex, asks, side), i32),
            pltpu.VMEM((n_ex, asks, side), i32),
            pltpu.VMEM((n_ft, slot_rows, side), i32),
            pltpu.VMEM((n_ft, slot_rows, side), i32),
            pltpu.VMEM((n_ex, ask_rows, side), bf16),
            pltpu.VMEM((n_ex, ask_rows, side), bf16),
            pltpu.VMEM((n_ft, slot_rows, side), f32),
            pltpu.VMEM((n_ft, slot_rows, side), f32),
            pltpu.VMEM((n_ft, slot_rows, side), f32),
            pltpu.VMEM((n_ft, slot_rows, side), f32),
            pltpu.VMEM((n_ex, ask_rows, side), f32),
            pltpu.VMEM((n_ex, ask_rows, side), f32),
            pltpu.VMEM((n_ex * ask_rows, side), f32),
            pltpu.VMEM((n_ft * slot_rows, side), f32),
            pltpu.VMEM((col_blocks * num_vecs, n_ex * ask_rows), bf16),
            pltpu.VMEM((num_vecs * row_blocks, n_ft * slot_rows), bf16),
            pltpu.VMEM((n_ft * slot_rows, side), bf16),
            pltpu.SemaphoreType.DMA((2,)),
        ] + [pltpu.SemaphoreType.DMA((n,)) for n in pairs for _ in range(2)],
        compiler_params=pltpu.CompilerParams(collective_id=0, has_side_effects=True),
    )(
        tile_count, tile_cslot, tile_rslot, need_cols, fold_rows,
        weights.reshape(row_blocks, side), tiles,
        directions.reshape(col_blocks * num_vecs, side),
    )
    return out.reshape(directions.shape)


def solution(mesh):
    return jax.shard_map(
        local,
        mesh=mesh,
        in_specs=(
            P(("ex", "ft"), None, None),
            P(("ex", "ft")),
            P(("ex", "ft")),
            P(("ex", "ft")),
            P(("ex", "ft"), None, None),
            P(("ex", "ft"), None, None),
            P("ft", "ex", None),
            P("ex", "ft", None, None),
        ),
        out_specs=P("ex", "ft", None, None),
        check_vma=False,
    )
```

```python
import functools
import jax
import jax.numpy as jnp
from jax import lax
from jax.experimental import pallas as pl
from jax.experimental.pallas import tpu as pltpu
from jax.sharding import PartitionSpec as P

scale_back = 4.0
tile_batch = 8


def partner(me, d, n):
    if n & (n - 1):
        return lax.rem(me + d, n)
    other, bit = me, 1
    while bit < n:
        if d & bit:
            other = other + bit * (1 - 2 * (me // bit % 2))
        bit *= 2
    return other


def exchange(axis, n, me, out_ref, in_ref, send_sem, recv_sem):
    copies = []
    for d in range(n - 1, 0, -1):
        peer = partner(me, d, n)
        copy = pltpu.make_async_remote_copy(
            src_ref=out_ref.at[peer],
            dst_ref=in_ref.at[me],
            send_sem=send_sem.at[d],
            recv_sem=recv_sem.at[d],
            device_id={axis: peer},
            device_id_type=pl.DeviceIdType.MESH,
        )
        copy.start()
        copies.append(copy)
    return copies


def split_three(x):
    high = x.astype(jnp.bfloat16)
    rest = x - high.astype(jnp.float32)
    middle = rest.astype(jnp.bfloat16)
    low = (rest - middle.astype(jnp.float32)).astype(jnp.bfloat16)
    return jnp.concatenate([high, middle, low], axis=0)


def kernel(
    n_ex, n_ft, num_vecs,
    count_ref, cslot_hbm, rslot_hbm, need_hbm, fold_hbm, weight_hbm, tiles_hbm, dir_hbm,
    out_ref,
    cslot_ref, rslot_ref, need_ref, fold_ref, weight_ref,
    col_base, row_base, col_live, row_live,
    tiles_v, dir_v, need_out, need_in, fold_out, fold_in, vec_out, vec_in,
    mar_out, mar_in, sc_out, sc_in, cur_out, cur_in,
    col_f, row_f, spread, collect, place, local_sem, *sems,
):
    f32, bf16, i32 = jnp.float32, jnp.bfloat16, jnp.int32
    ex_me, ft_me = lax.axis_index("ex"), lax.axis_index("ft")
    asks, slots = need_ref.shape[2], fold_ref.shape[1]
    row_blocks = weight_ref.shape[0]
    slot_count, side = tiles_v.shape[0], tiles_v.shape[1]
    ask_rows, slot_rows = num_vecs * asks, num_vecs * slots
    all_asks, all_slots = n_ex * ask_rows, n_ft * slot_rows

    barrier = pltpu.get_barrier_semaphore()
    for axis, n, me in (("ex", n_ex, ex_me), ("ft", n_ft, ft_me)):
        for d in range(n - 1, 0, -1):
            pl.semaphore_signal(barrier, inc=1, device_id={axis: partner(me, d, n)},
                                device_id_type=pl.DeviceIdType.MESH)

    fetched = []
    for index, (source, target) in enumerate((
        (need_hbm, need_ref), (fold_hbm, fold_ref),
        (cslot_hbm, cslot_ref), (rslot_hbm, rslot_ref), (dir_hbm, dir_v),
        (weight_hbm, weight_ref), (tiles_hbm, tiles_v),
    )):
        fetched.append(pltpu.make_async_copy(source, target, local_sem.at[index]))
        fetched[-1].start()
    need_copy, fold_copy, cslot_copy, rslot_copy, dir_copy, weight_copy, tile_copy = fetched

    need_copy.wait()
    sub = lax.broadcasted_iota(i32, (asks, side), 0)
    for o in range(n_ex):
        block = jnp.zeros((asks, side), i32)
        for j in range(asks):
            block = jnp.where(sub == j, need_ref[0, o, j], block)
        need_out[o] = block
    pl.semaphore_wait(barrier, n_ex - 1 + n_ft - 1)

    need_copies = exchange("ex", n_ex, ex_me, need_out, need_in, sems[0], sems[1])
    need_in[ex_me] = need_out[ex_me]

    fold_copy.wait()
    sub = lax.broadcasted_iota(i32, (slot_rows, side), 0)
    for q in range(n_ft):
        block = jnp.zeros((slot_rows, side), i32)
        for i in range(slots):
            block = jnp.where(sub % slots == i, fold_ref[0, i, q], block)
        fold_out[q] = block + (sub // slots) * row_blocks

    cslot_copy.wait()
    rslot_copy.wait()
    live = count_ref[0]

    @pl.loop(0, slot_count // tile_batch)
    def _(step):
        for u in range(tile_batch):
            t = step * tile_batch + u
            c, r = cslot_ref[t], rslot_ref[t]
            col_base[t] = lax.div(c, asks) * ask_rows + lax.rem(c, asks)
            row_base[t] = lax.div(r, slots) * slot_rows + lax.rem(r, slots)
            col_live[t] = jnp.where(t < live, c, -1)
            row_live[t] = jnp.where(t < live, r, -1)

    dir_copy.wait()
    dir_bf = dir_v[...].astype(bf16)
    col_rows = dir_v.shape[0]
    for copy in need_copies:
        copy.wait()
    asked = need_in[...]
    asked = jnp.concatenate([asked * num_vecs + k for k in range(num_vecs)], axis=1)
    asked = asked.reshape(all_asks, side)
    lane = lax.broadcasted_iota(i32, (all_asks, side), 1)
    hot = jnp.concatenate(
        [jnp.where(lane + base == asked, 1.0, 0.0) for base in range(0, col_rows, side)], axis=1
    )
    picked = jnp.dot(hot.astype(bf16), dir_bf, preferred_element_type=f32)
    vec_out[...] = picked.astype(bf16).reshape(vec_out.shape)
    vec_copies = exchange("ex", n_ex, ex_me, vec_out, vec_in, sems[4], sems[5])
    vec_in[ex_me] = vec_out[ex_me]
    fold_copies = exchange("ft", n_ft, ft_me, fold_out, fold_in, sems[2], sems[3])
    fold_in[ft_me] = fold_out[ft_me]

    spread[...] = hot.T.astype(bf16)
    for copy in fold_copies:
        copy.wait()
    lane = lax.broadcasted_iota(i32, (all_slots, side), 1)
    rows_hot = jnp.where(fold_in[...].reshape(all_slots, side) == lane, 1.0, 0.0)
    place[...] = rows_hot.astype(bf16)
    collect[...] = rows_hot.T[: num_vecs * row_blocks].astype(bf16)
    weight_copy.wait()
    weight = jnp.concatenate([weight_ref[...]] * num_vecs, axis=0)

    for copy in vec_copies:
        copy.wait()
    col_f[...] = vec_in[...].reshape(all_asks, side).astype(f32)
    tile_copy.wait()

    row_id = lax.broadcasted_iota(i32, (all_slots, side), 0)
    row_slot = (row_id // slot_rows) * slots + row_id % slots
    half = lax.broadcasted_iota(i32, (slot_rows, side), 0) // slots

    def forward(step, total):
        lefts, rights = [], []
        for u in range(tile_batch):
            t = step * tile_batch + u
            base, r = col_base[t], row_live[t]
            value = jnp.broadcast_to(col_f[pl.ds(base, 1), :], (slot_rows, side))
            for k in range(1, num_vecs):
                other = jnp.broadcast_to(col_f[pl.ds(base + k * asks, 1), :], (slot_rows, side))
                value = jnp.where(half >= k, other, value)
            value = jnp.concatenate([value] * n_ft, axis=0)
            lefts.append(jnp.where(row_slot == r, value, 0.0).astype(bf16))
            rights.append(tiles_v[t])
        return total + lax.dot_general(
            jnp.concatenate(lefts, axis=1), jnp.concatenate(rights, axis=1),
            (((1,), (1,)), ((), ())), preferred_element_type=f32,
        )

    part = lax.fori_loop(0, slot_count // tile_batch, forward, jnp.zeros((all_slots, side), f32))
    mar_out[...] = part.reshape(mar_out.shape)
    mar_copies = exchange("ft", n_ft, ft_me, mar_out, mar_in, sems[6], sems[7])
    mar_in[ft_me] = mar_out[ft_me]
    for copy in mar_copies:
        copy.wait()
    pieces = split_three(mar_in[...].reshape(all_slots, side))
    gather = collect[...]
    margins = jnp.dot(
        jnp.concatenate([gather] * 3, axis=1), pieces, preferred_element_type=f32
    )
    scaled = weight * margins
    filler = jnp.zeros((side - num_vecs * row_blocks, side), f32)
    scaled = jnp.concatenate([scaled, filler], axis=0).astype(bf16)
    answer = jnp.dot(place[...], scaled, preferred_element_type=f32)
    sc_out[...] = answer.astype(sc_out.dtype).reshape(sc_out.shape)
    sc_copies = exchange("ft", n_ft, ft_me, sc_out, sc_in, sems[8], sems[9])
    sc_in[ft_me] = sc_out[ft_me]
    for copy in sc_copies:
        copy.wait()
    row_f[...] = sc_in[...].astype(f32).reshape(all_slots, side)

    col_id = lax.broadcasted_iota(i32, (all_asks, side), 0)
    col_slot = (col_id // ask_rows) * asks + col_id % asks

    def backward(step, total):
        lefts, rights = [], []
        for u in range(tile_batch):
            t = step * tile_batch + u
            base, c = row_base[t], col_live[t]
            values = [
                jnp.broadcast_to(row_f[pl.ds(base + k * slots, 1), :], (asks, side))
                for k in range(num_vecs)
            ]
            value = jnp.concatenate(values * n_ex, axis=0)
            lefts.append(jnp.where(col_slot == c, value, 0.0).astype(bf16))
            rights.append(tiles_v[t])
        return total + jnp.dot(
            jnp.concatenate(lefts, axis=1), jnp.concatenate(rights, axis=0),
            preferred_element_type=f32,
        )

    part = lax.fori_loop(0, slot_count // tile_batch, backward, jnp.zeros((all_asks, side), f32))
    cur_out[...] = part.reshape(cur_out.shape)
    cur_copies = exchange("ex", n_ex, ex_me, cur_out, cur_in, sems[10], sems[11])
    cur_in[ex_me] = cur_out[ex_me]
    for copy in cur_copies:
        copy.wait()
    pieces = split_three(cur_in[...].reshape(all_asks, side))
    scatter = spread[...]
    curvature = jnp.dot(
        jnp.concatenate([scatter] * 3, axis=1), pieces, preferred_element_type=f32
    )
    out_ref[...] = curvature


def local(tiles, tile_count, tile_cslot, tile_rslot, need_cols, fold_rows, weights, directions):
    n_ex, n_ft = lax.axis_size("ex"), lax.axis_size("ft")
    side = tiles.shape[1]
    col_blocks, num_vecs = directions.shape[0], directions.shape[2]
    row_blocks = weights.shape[0]
    asks, slots = need_cols.shape[2], fold_rows.shape[2]
    ask_rows, slot_rows = num_vecs * asks, num_vecs * slots
    f32, bf16, i32 = jnp.float32, jnp.bfloat16, jnp.int32
    vmem = pl.BlockSpec(memory_space=pltpu.VMEM)
    hbm = pl.BlockSpec(memory_space=pltpu.HBM)
    pairs = [n_ex, n_ft, n_ex, n_ft, n_ft, n_ex]
    own = directions.reshape(col_blocks * num_vecs, side)
    out = pl.pallas_call(
        functools.partial(kernel, n_ex, n_ft, num_vecs),
        out_shape=jax.ShapeDtypeStruct((col_blocks * num_vecs, side), f32),
        in_specs=[pl.BlockSpec(memory_space=pltpu.SMEM)] + [hbm] * 7,
        out_specs=vmem,
        scratch_shapes=[
            pltpu.SMEM(tile_cslot.shape, i32),
            pltpu.SMEM(tile_rslot.shape, i32),
            pltpu.SMEM(need_cols.shape, i32),
            pltpu.SMEM((1, slots, n_ft), i32),
            pltpu.VMEM((row_blocks, side), f32),
        ] + [pltpu.SMEM(tile_cslot.shape, i32)] * 4 + [
            pltpu.VMEM(tiles.shape, bf16),
            pltpu.VMEM((col_blocks * num_vecs, side), f32),
            pltpu.VMEM((n_ex, asks, side), i32),
            pltpu.VMEM((n_ex, asks, side), i32),
            pltpu.VMEM((n_ft, slot_rows, side), i32),
            pltpu.VMEM((n_ft, slot_rows, side), i32),
            pltpu.VMEM((n_ex, ask_rows, side), bf16),
            pltpu.VMEM((n_ex, ask_rows, side), bf16),
            pltpu.VMEM((n_ft, slot_rows, side), f32),
            pltpu.VMEM((n_ft, slot_rows, side), f32),
            pltpu.VMEM((n_ft, slot_rows, side), f32),
            pltpu.VMEM((n_ft, slot_rows, side), f32),
            pltpu.VMEM((n_ex, ask_rows, side), f32),
            pltpu.VMEM((n_ex, ask_rows, side), f32),
            pltpu.VMEM((n_ex * ask_rows, side), f32),
            pltpu.VMEM((n_ft * slot_rows, side), f32),
            pltpu.VMEM((col_blocks * num_vecs, n_ex * ask_rows), bf16),
            pltpu.VMEM((num_vecs * row_blocks, n_ft * slot_rows), bf16),
            pltpu.VMEM((n_ft * slot_rows, side), bf16),
            pltpu.SemaphoreType.DMA((7,)),
        ] + [pltpu.SemaphoreType.DMA((n,)) for n in pairs for _ in range(2)],
        compiler_params=pltpu.CompilerParams(collective_id=0, has_side_effects=True, vmem_limit_bytes=8 << 20),
    )(tile_count, *(pltpu.with_memory_space_constraint(x, pltpu.HBM) for x in (
        tile_cslot, tile_rslot, need_cols, fold_rows.transpose(0, 2, 1),
        weights.reshape(row_blocks, side), tiles, own,
    )))
    return (own + scale_back * out).reshape(directions.shape)


def solution(mesh):
    return jax.shard_map(
        local,
        mesh=mesh,
        in_specs=(
            P(("ex", "ft"), None, None),
            P(("ex", "ft")),
            P(("ex", "ft")),
            P(("ex", "ft")),
            P(("ex", "ft"), None, None),
            P(("ex", "ft"), None, None),
            P("ft", "ex", None),
            P("ex", "ft", None, None),
        ),
        out_specs=P("ex", "ft", None, None),
        check_vma=False,
    )
```

```python
import functools
import jax
import jax.numpy as jnp
from jax import lax
from jax.experimental import pallas as pl
from jax.experimental.pallas import tpu as pltpu
from jax.sharding import PartitionSpec as P

scale_back = 4.0
tile_batch = 32


def partner(me, d, n):
    if n & (n - 1):
        return lax.rem(me + d, n)
    other, bit = me, 1
    while bit < n:
        if d & bit:
            other = other + bit * (1 - 2 * (me // bit % 2))
        bit *= 2
    return other


def exchange(axis, n, me, out_ref, in_ref, send_sem, recv_sem, shared=False):
    copies = []
    for d in range(n - 1, 0, -1):
        peer = partner(me, d, n)
        copy = pltpu.make_async_remote_copy(
            src_ref=out_ref if shared else out_ref.at[peer],
            dst_ref=in_ref.at[me],
            send_sem=send_sem.at[d],
            recv_sem=recv_sem.at[d],
            device_id={axis: peer},
            device_id_type=pl.DeviceIdType.MESH,
        )
        copy.start()
        copies.append(copy)
    return copies


def split_three(x):
    high = x.astype(jnp.bfloat16)
    rest = x - high.astype(jnp.float32)
    middle = rest.astype(jnp.bfloat16)
    low = (rest - middle.astype(jnp.float32)).astype(jnp.bfloat16)
    return high, middle, low


def kernel(
    n_ex, n_ft, num_vecs,
    count_ref, cslot_hbm, rslot_hbm, need_hbm, fold_hbm, weight_hbm, tiles_hbm, dir_hbm,
    out_ref,
    cslot_ref, rslot_ref, need_ref, fold_ref, weight_ref,
    col_base, row_base, col_live, row_live,
    tiles_v, dir_v, need_out, need_in, own_code, info_out, info_in, vec_out, vec_in,
    mar_out, mar_in, cur_out, cur_in,
    col_f, row_f, spread, collect, weight_own, local_sem, *sems,
):
    f32, bf16, i32 = jnp.float32, jnp.bfloat16, jnp.int32
    ex_me, ft_me = lax.axis_index("ex"), lax.axis_index("ft")
    asks, slots = need_ref.shape[2], fold_ref.shape[1]
    row_blocks = weight_ref.shape[0]
    slot_count, side = tiles_v.shape[0], tiles_v.shape[1]
    ask_rows, slot_rows = num_vecs * asks, num_vecs * slots
    all_asks, all_slots = n_ex * ask_rows, n_ft * slot_rows

    barrier = pltpu.get_barrier_semaphore()
    for axis, n, me in (("ex", n_ex, ex_me), ("ft", n_ft, ft_me)):
        for d in range(n - 1, 0, -1):
            pl.semaphore_signal(barrier, inc=1, device_id={axis: partner(me, d, n)},
                                device_id_type=pl.DeviceIdType.MESH)

    fetched = []
    for index, (source, target) in enumerate((
        (need_hbm, need_ref), (fold_hbm, fold_ref),
        (cslot_hbm, cslot_ref), (rslot_hbm, rslot_ref), (dir_hbm, dir_v),
        (weight_hbm, weight_ref), (tiles_hbm, tiles_v),
    )):
        fetched.append(pltpu.make_async_copy(source, target, local_sem.at[index]))
        fetched[-1].start()
    need_copy, fold_copy, cslot_copy, rslot_copy, dir_copy, weight_copy, tile_copy = fetched

    need_copy.wait()
    sub = lax.broadcasted_iota(i32, (asks, side), 0)
    for o in range(n_ex):
        block = jnp.zeros((asks, side), i32)
        for j in range(asks):
            block = jnp.where(sub == j, need_ref[0, o, j], block)
        need_out[o] = block
    pl.semaphore_wait(barrier, n_ex - 1 + n_ft - 1)

    need_copies = exchange("ex", n_ex, ex_me, need_out, need_in, sems[0], sems[1])
    need_in[ex_me] = need_out[ex_me]

    fold_copy.wait()
    weight_copy.wait()
    width = own_code.shape[1]
    sub = lax.broadcasted_iota(i32, (slot_rows, width), 0)
    lane = lax.broadcasted_iota(i32, (8, width), 1) % all_slots
    codes = (lane % slot_rows) // slots * n_ft * row_blocks + lane // slot_rows * row_blocks
    lane_slot = lane // slot_rows * slots + lane % slots
    listed = jnp.zeros((8, width), i32)
    for q in range(n_ft):
        block = jnp.zeros((slot_rows, width), i32)
        for i in range(slots):
            block = jnp.where(sub % slots == i, fold_ref[0, i, q], block)
            listed = jnp.where(lane_slot == q * slots + i, fold_ref[0, i, q], listed)
        own_code[pl.ds(q * slot_rows, slot_rows), :] = block + q * row_blocks
    info_out[pl.ds(0, row_blocks), pl.ds(0, side)] = weight_ref[...]
    info_out[pl.ds(row_blocks, 8), :] = (listed + codes).astype(f32)

    cslot_copy.wait()
    rslot_copy.wait()
    live = count_ref[0]

    @pl.loop(0, slot_count // tile_batch)
    def _(step):
        for u in range(tile_batch):
            t = step * tile_batch + u
            c, r = cslot_ref[t], rslot_ref[t]
            col_base[t] = lax.div(c, asks) * ask_rows + lax.rem(c, asks)
            row_base[t] = lax.div(r, slots) * slot_rows + lax.rem(r, slots)
            col_live[t] = jnp.where(t < live, c, -1)
            row_live[t] = jnp.where(t < live, r, -1)

    dir_copy.wait()
    dir_bf = dir_v[...].astype(bf16)
    col_rows = dir_v.shape[0]
    for copy in need_copies:
        copy.wait()
    asked = need_in[...]
    asked = jnp.concatenate([asked * num_vecs + k for k in range(num_vecs)], axis=1)
    asked = asked.reshape(all_asks, side)
    lane = lax.broadcasted_iota(i32, (all_asks, side), 1)
    hot = jnp.concatenate(
        [jnp.where(lane + base == asked, 1.0, 0.0) for base in range(0, col_rows, side)], axis=1
    )
    picked = jnp.dot(hot.astype(bf16), dir_bf, preferred_element_type=f32)
    vec_out[...] = picked.astype(bf16).reshape(vec_out.shape)
    vec_copies = exchange("ex", n_ex, ex_me, vec_out, vec_in, sems[4], sems[5])
    vec_in[ex_me] = vec_out[ex_me]
    info_copies = exchange(
        "ft", n_ft, ft_me, info_out, info_in, sems[2], sems[3], shared=True
    )
    info_in[ft_me] = info_out[...]

    spread[...] = hot.T.astype(bf16)
    for copy in info_copies:
        copy.wait()
    code = own_code[...]
    row_total = n_ft * row_blocks
    lane = lax.broadcasted_iota(i32, (all_slots, row_total), 1)
    hot = jnp.where(code[:, :row_total] == lane, 1.0, 0.0).astype(bf16)
    weights = info_in[:, pl.ds(0, row_blocks), pl.ds(0, side)].reshape(row_total, side)
    weight_own[...] = sum(
        jnp.dot(hot, piece, preferred_element_type=f32) for piece in split_three(weights)
    )
    sub = lax.broadcasted_iota(i32, (all_slots, width), 0) % slot_rows // slots
    code = (code + sub * row_total).astype(f32)
    group = width // all_slots
    lane = lax.broadcasted_iota(i32, (1, width), 1) // all_slots
    for g in range(n_ft // group):
        line = info_in[g * group, pl.ds(row_blocks, 1), :]
        for h in range(1, group):
            other = info_in[g * group + h, pl.ds(row_blocks, 1), :]
            line = jnp.where(lane == h, other, line)
        collect[:, pl.ds(g * width, width)] = jnp.where(code == line, 1.0, 0.0).astype(bf16)

    for copy in vec_copies:
        copy.wait()
    col_f[...] = vec_in[...].reshape(all_asks, side).astype(f32)
    tile_copy.wait()

    row_id = lax.broadcasted_iota(i32, (all_slots, side), 0)
    row_slot = (row_id // slot_rows) * slots + row_id % slots
    half = lax.broadcasted_iota(i32, (slot_rows, side), 0) // slots

    def forward(step, total):
        lefts, rights = [], []
        for u in range(tile_batch):
            t = step * tile_batch + u
            base, r = col_base[t], row_live[t]
            value = jnp.broadcast_to(col_f[pl.ds(base, 1), :], (slot_rows, side))
            for k in range(1, num_vecs):
                other = jnp.broadcast_to(col_f[pl.ds(base + k * asks, 1), :], (slot_rows, side))
                value = jnp.where(half >= k, other, value)
            value = jnp.concatenate([value] * n_ft, axis=0)
            lefts.append(jnp.where(row_slot == r, value, 0.0).astype(bf16))
            rights.append(tiles_v[t])
        return total + lax.dot_general(
            jnp.concatenate(lefts, axis=1), jnp.concatenate(rights, axis=1),
            (((1,), (1,)), ((), ())), preferred_element_type=f32,
        )

    part = lax.fori_loop(0, slot_count // tile_batch, forward, jnp.zeros((all_slots, side), f32))
    mar_out[...] = part.astype(bf16)
    mar_copies = exchange("ft", n_ft, ft_me, mar_out, mar_in, sems[6], sems[7], shared=True)
    mar_in[ft_me] = mar_out[...]
    for copy in mar_copies:
        copy.wait()
    margins = jnp.dot(
        collect[...], mar_in[...].reshape(n_ft * all_slots, side), preferred_element_type=f32
    )
    row_f[...] = (weight_own[...] * margins).astype(bf16).astype(f32)

    col_id = lax.broadcasted_iota(i32, (all_asks, side), 0)
    col_slot = (col_id // ask_rows) * asks + col_id % asks

    def backward(step, total):
        lefts, rights = [], []
        for u in range(tile_batch):
            t = step * tile_batch + u
            base, c = row_base[t], col_live[t]
            values = [
                jnp.broadcast_to(row_f[pl.ds(base + k * slots, 1), :], (asks, side))
                for k in range(num_vecs)
            ]
            value = jnp.concatenate(values * n_ex, axis=0)
            lefts.append(jnp.where(col_slot == c, value, 0.0).astype(bf16))
            rights.append(tiles_v[t])
        return total + jnp.dot(
            jnp.concatenate(lefts, axis=1), jnp.concatenate(rights, axis=0),
            preferred_element_type=f32,
        )

    part = lax.fori_loop(0, slot_count // tile_batch, backward, jnp.zeros((all_asks, side), f32))
    cur_out[...] = part.reshape(cur_out.shape)
    cur_copies = exchange("ex", n_ex, ex_me, cur_out, cur_in, sems[8], sems[9])
    cur_in[ex_me] = cur_out[ex_me]
    for copy in cur_copies:
        copy.wait()
    pieces = jnp.concatenate(split_three(cur_in[...].reshape(all_asks, side)), axis=0)
    scatter = spread[...]
    curvature = jnp.dot(
        jnp.concatenate([scatter] * 3, axis=1), pieces, preferred_element_type=f32
    )
    out_ref[...] = curvature


def local(tiles, tile_count, tile_cslot, tile_rslot, need_cols, fold_rows, weights, directions):
    n_ex, n_ft = lax.axis_size("ex"), lax.axis_size("ft")
    side = tiles.shape[1]
    col_blocks, num_vecs = directions.shape[0], directions.shape[2]
    row_blocks = weights.shape[0]
    asks, slots = need_cols.shape[2], fold_rows.shape[2]
    ask_rows, slot_rows = num_vecs * asks, num_vecs * slots
    f32, bf16, i32 = jnp.float32, jnp.bfloat16, jnp.int32
    vmem = pl.BlockSpec(memory_space=pltpu.VMEM)
    hbm = pl.BlockSpec(memory_space=pltpu.HBM)
    pairs = [n_ex, n_ft, n_ex, n_ft, n_ex]
    all_slots = n_ft * slot_rows
    width = max(all_slots, 128)
    own = directions.reshape(col_blocks * num_vecs, side)
    out = pl.pallas_call(
        functools.partial(kernel, n_ex, n_ft, num_vecs),
        out_shape=jax.ShapeDtypeStruct((col_blocks * num_vecs, side), f32),
        in_specs=[pl.BlockSpec(memory_space=pltpu.SMEM)] + [hbm] * 7,
        out_specs=vmem,
        scratch_shapes=[
            pltpu.SMEM(tile_cslot.shape, i32),
            pltpu.SMEM(tile_rslot.shape, i32),
            pltpu.SMEM(need_cols.shape, i32),
            pltpu.SMEM((1, slots, n_ft), i32),
            pltpu.VMEM((row_blocks, side), f32),
        ] + [pltpu.SMEM(tile_cslot.shape, i32)] * 4 + [
            pltpu.VMEM(tiles.shape, bf16),
            pltpu.VMEM((col_blocks * num_vecs, side), f32),
            pltpu.VMEM((n_ex, asks, side), i32),
            pltpu.VMEM((n_ex, asks, side), i32),
            pltpu.VMEM((all_slots, width), i32),
            pltpu.VMEM((row_blocks + 8, width), f32),
            pltpu.VMEM((n_ft, row_blocks + 8, width), f32),
            pltpu.VMEM((n_ex, ask_rows, side), bf16),
            pltpu.VMEM((n_ex, ask_rows, side), bf16),
            pltpu.VMEM((all_slots, side), bf16),
            pltpu.VMEM((n_ft, all_slots, side), bf16),
            pltpu.VMEM((n_ex, ask_rows, side), f32),
            pltpu.VMEM((n_ex, ask_rows, side), f32),
            pltpu.VMEM((n_ex * ask_rows, side), f32),
            pltpu.VMEM((n_ft * slot_rows, side), f32),
            pltpu.VMEM((col_blocks * num_vecs, n_ex * ask_rows), bf16),
            pltpu.VMEM((all_slots, n_ft * all_slots), bf16),
            pltpu.VMEM((all_slots, side), f32),
            pltpu.SemaphoreType.DMA((7,)),
        ] + [pltpu.SemaphoreType.DMA((n,)) for n in pairs for _ in range(2)],
        compiler_params=pltpu.CompilerParams(collective_id=0, has_side_effects=True, vmem_limit_bytes=24 << 20),
    )(tile_count, *(pltpu.with_memory_space_constraint(x, pltpu.HBM) for x in (
        tile_cslot, tile_rslot, need_cols, fold_rows.transpose(0, 2, 1),
        weights.reshape(row_blocks, side), tiles, own,
    )))
    return (own + scale_back * out).reshape(directions.shape)


def solution(mesh):
    return jax.shard_map(
        local,
        mesh=mesh,
        in_specs=(
            P(("ex", "ft"), None, None),
            P(("ex", "ft")),
            P(("ex", "ft")),
            P(("ex", "ft")),
            P(("ex", "ft"), None, None),
            P(("ex", "ft"), None, None),
            P("ft", "ex", None),
            P("ex", "ft", None, None),
        ),
        out_specs=P("ex", "ft", None, None),
        check_vma=False,
    )
```

```python
import functools
import jax
import jax.numpy as jnp
from jax import lax
from jax.experimental import pallas as pl
from jax.experimental.pallas import tpu as pltpu
from jax.sharding import PartitionSpec as P

scale_back = 4.0
tile_batch = 48


def partner(me, d, n):
    if n & (n - 1):
        return lax.rem(me + d, n)
    other, bit = me, 1
    while bit < n:
        if d & bit:
            other = other + bit * (1 - 2 * (me // bit % 2))
        bit *= 2
    return other


def exchange(axis, n, me, out_ref, in_ref, send_sem, recv_sem, shared=False):
    copies = []
    for d in range(n - 1, 0, -1):
        peer = partner(me, d, n)
        copy = pltpu.make_async_remote_copy(
            src_ref=out_ref if shared else out_ref.at[peer],
            dst_ref=in_ref.at[me],
            send_sem=send_sem.at[d],
            recv_sem=recv_sem.at[d],
            device_id={axis: peer},
            device_id_type=pl.DeviceIdType.MESH,
        )
        copy.start()
        copies.append(copy)
    return copies


def split_three(x):
    high = x.astype(jnp.bfloat16)
    rest = x - high.astype(jnp.float32)
    middle = rest.astype(jnp.bfloat16)
    low = (rest - middle.astype(jnp.float32)).astype(jnp.bfloat16)
    return high, middle, low


def kernel(
    n_ex, n_ft, num_vecs,
    count_ref, cslot_hbm, rslot_hbm, need_hbm, fold_hbm, weight_hbm, tiles_hbm, dir_hbm,
    out_ref,
    cslot_ref, rslot_ref, need_ref, fold_ref, weight_ref,
    col_base, row_base, col_live, row_live,
    tiles_v, dir_v, need_out, need_in, own_code, info_out, info_in, vec_out, vec_in,
    mar_out, mar_in, cur_out, cur_in,
    col_f, row_f, spread, collect, weight_own, local_sem, *sems,
):
    f32, bf16, i32 = jnp.float32, jnp.bfloat16, jnp.int32
    ex_me, ft_me = lax.axis_index("ex"), lax.axis_index("ft")
    asks, slots = need_ref.shape[2], fold_ref.shape[1]
    row_blocks = weight_ref.shape[0]
    slot_count, side = tiles_v.shape[0], tiles_v.shape[1]
    ask_rows, slot_rows = num_vecs * asks, num_vecs * slots
    all_asks, all_slots = n_ex * ask_rows, n_ft * slot_rows

    barrier = pltpu.get_barrier_semaphore()
    for axis, n, me in (("ex", n_ex, ex_me), ("ft", n_ft, ft_me)):
        for d in range(n - 1, 0, -1):
            pl.semaphore_signal(barrier, inc=1, device_id={axis: partner(me, d, n)},
                                device_id_type=pl.DeviceIdType.MESH)

    fetched = []
    for index, (source, target) in enumerate((
        (need_hbm, need_ref), (fold_hbm, fold_ref),
        (cslot_hbm, cslot_ref), (rslot_hbm, rslot_ref), (dir_hbm, dir_v),
        (weight_hbm, weight_ref), (tiles_hbm, tiles_v),
    )):
        fetched.append(pltpu.make_async_copy(source, target, local_sem.at[index]))
        fetched[-1].start()
    need_copy, fold_copy, cslot_copy, rslot_copy, dir_copy, weight_copy, tile_copy = fetched

    need_copy.wait()
    lane = lax.broadcasted_iota(i32, (1, side), 1)
    for o in range(n_ex):
        line = jnp.zeros((1, side), i32)
        for j in range(asks):
            line = jnp.where(lane == j, need_ref[0, o, j], line)
        need_out[o] = line

    pl.semaphore_wait(barrier, n_ex - 1 + n_ft - 1)

    need_copies = exchange("ex", n_ex, ex_me, need_out, need_in, sems[0], sems[1])
    need_in[ex_me] = need_out[ex_me]

    fold_copy.wait()
    weight_copy.wait()
    width = own_code.shape[1]
    sub = lax.broadcasted_iota(i32, (slot_rows, width), 0)
    lane = lax.broadcasted_iota(i32, (8, width), 1) % all_slots
    codes = (lane % slot_rows) // slots * n_ft * row_blocks + lane // slot_rows * row_blocks
    lane_slot = lane // slot_rows * slots + lane % slots
    listed = jnp.zeros((8, width), i32)
    for q in range(n_ft):
        block = jnp.zeros((slot_rows, width), i32)
        for i in range(slots):
            block = jnp.where(sub % slots == i, fold_ref[0, i, q], block)
            listed = jnp.where(lane_slot == q * slots + i, fold_ref[0, i, q], listed)
        own_code[pl.ds(q * slot_rows, slot_rows), :] = block + q * row_blocks
    info_out[pl.ds(0, row_blocks), pl.ds(0, side)] = weight_ref[...]
    info_out[pl.ds(row_blocks, 8), :] = (listed + codes).astype(f32)

    cslot_copy.wait()
    rslot_copy.wait()
    live = count_ref[0]

    @pl.loop(0, slot_count // tile_batch)
    def _(step):
        for u in range(tile_batch):
            t = step * tile_batch + u
            c, r = cslot_ref[t], rslot_ref[t]
            col_base[t] = lax.div(c, asks) * ask_rows + lax.rem(c, asks)
            row_base[t] = lax.div(r, slots) * slot_rows + lax.rem(r, slots)
            col_live[t] = jnp.where(t < live, c, -1)
            row_live[t] = jnp.where(t < live, r, -1)

    dir_copy.wait()
    dir_bf = dir_v[...].astype(bf16)
    col_rows = dir_v.shape[0]
    for copy in need_copies:
        copy.wait()
    asked = jnp.broadcast_to(need_in[...].astype(f32), (n_ex, asks, side))
    sub = lax.broadcasted_iota(i32, (n_ex, asks, side), 1)
    lane = lax.broadcasted_iota(i32, (n_ex, asks, side), 2)
    asked = jnp.sum(jnp.where(sub == lane, asked, 0.0), axis=2, keepdims=True)
    asked = jnp.broadcast_to(asked, (n_ex, asks, side)).astype(i32)
    asked = jnp.concatenate([asked * num_vecs + k for k in range(num_vecs)], axis=1)
    asked = asked.reshape(all_asks, side)
    lane = lax.broadcasted_iota(i32, (all_asks, side), 1)
    hot = jnp.concatenate(
        [jnp.where(lane + base == asked, 1.0, 0.0) for base in range(0, col_rows, side)], axis=1
    )
    picked = jnp.dot(hot.astype(bf16), dir_bf, preferred_element_type=f32)
    vec_out[...] = picked.astype(bf16).reshape(vec_out.shape)
    vec_copies = exchange("ex", n_ex, ex_me, vec_out, vec_in, sems[4], sems[5])
    vec_in[ex_me] = vec_out[ex_me]
    info_copies = exchange(
        "ft", n_ft, ft_me, info_out, info_in, sems[2], sems[3], shared=True
    )
    info_in[ft_me] = info_out[...]

    spread[...] = hot.T.astype(bf16)
    for copy in info_copies:
        copy.wait()
    code = own_code[...]
    row_total = n_ft * row_blocks
    lane = lax.broadcasted_iota(i32, (all_slots, row_total), 1)
    hot = jnp.where(code[:, :row_total] == lane, 1.0, 0.0).astype(bf16)
    weights = info_in[:, pl.ds(0, row_blocks), pl.ds(0, side)].reshape(row_total, side)
    weight_own[...] = sum(
        jnp.dot(hot, piece, preferred_element_type=f32) for piece in split_three(weights)
    )
    sub = lax.broadcasted_iota(i32, (all_slots, width), 0) % slot_rows // slots
    code = (code + sub * row_total).astype(f32)
    group = width // all_slots
    lane = lax.broadcasted_iota(i32, (1, width), 1) // all_slots
    for g in range(n_ft // group):
        line = info_in[g * group, pl.ds(row_blocks, 1), :]
        for h in range(1, group):
            other = info_in[g * group + h, pl.ds(row_blocks, 1), :]
            line = jnp.where(lane == h, other, line)
        collect[:, pl.ds(g * width, width)] = jnp.where(code == line, 1.0, 0.0).astype(bf16)

    for copy in vec_copies:
        copy.wait()
    col_f[...] = vec_in[...].reshape(all_asks, side).astype(f32)
    tile_copy.wait()

    row_id = lax.broadcasted_iota(i32, (all_slots, side), 0)
    row_slot = (row_id // slot_rows) * slots + row_id % slots
    half = lax.broadcasted_iota(i32, (slot_rows, side), 0) // slots

    def forward(step, total):
        lefts, rights = [], []
        for u in range(tile_batch):
            t = step * tile_batch + u
            base, r = col_base[t], row_live[t]
            value = jnp.broadcast_to(col_f[pl.ds(base, 1), :], (slot_rows, side))
            for k in range(1, num_vecs):
                other = jnp.broadcast_to(col_f[pl.ds(base + k * asks, 1), :], (slot_rows, side))
                value = jnp.where(half >= k, other, value)
            value = jnp.concatenate([value] * n_ft, axis=0)
            lefts.append(jnp.where(row_slot == r, value, 0.0).astype(bf16))
            rights.append(tiles_v[t])
        return total + lax.dot_general(
            jnp.concatenate(lefts, axis=1), jnp.concatenate(rights, axis=1),
            (((1,), (1,)), ((), ())), preferred_element_type=f32,
        )

    part = lax.fori_loop(0, slot_count // tile_batch, forward, jnp.zeros((all_slots, side), f32))
    mar_out[...] = part.astype(bf16)
    mar_copies = exchange("ft", n_ft, ft_me, mar_out, mar_in, sems[6], sems[7], shared=True)
    mar_in[ft_me] = mar_out[...]
    for copy in mar_copies:
        copy.wait()
    margins = jnp.dot(
        collect[...], mar_in[...].reshape(n_ft * all_slots, side), preferred_element_type=f32
    )
    row_f[...] = (weight_own[...] * margins).astype(bf16).astype(f32)

    col_id = lax.broadcasted_iota(i32, (all_asks, side), 0)
    col_slot = (col_id // ask_rows) * asks + col_id % asks

    def backward(step, total):
        lefts, rights = [], []
        for u in range(tile_batch):
            t = step * tile_batch + u
            base, c = row_base[t], col_live[t]
            values = [
                jnp.broadcast_to(row_f[pl.ds(base + k * slots, 1), :], (asks, side))
                for k in range(num_vecs)
            ]
            value = jnp.concatenate(values * n_ex, axis=0)
            lefts.append(jnp.where(col_slot == c, value, 0.0).astype(bf16))
            rights.append(tiles_v[t])
        return total + jnp.dot(
            jnp.concatenate(lefts, axis=1), jnp.concatenate(rights, axis=0),
            preferred_element_type=f32,
        )

    part = lax.fori_loop(0, slot_count // tile_batch, backward, jnp.zeros((all_asks, side), f32))
    cur_out[...] = part.reshape(cur_out.shape)
    cur_copies = exchange("ex", n_ex, ex_me, cur_out, cur_in, sems[8], sems[9])
    cur_in[ex_me] = cur_out[ex_me]
    for copy in cur_copies:
        copy.wait()
    pieces = jnp.concatenate(split_three(cur_in[...].reshape(all_asks, side)), axis=0)
    scatter = spread[...]
    curvature = jnp.dot(
        jnp.concatenate([scatter] * 3, axis=1), pieces, preferred_element_type=f32
    )
    out_ref[...] = curvature


def local(tiles, tile_count, tile_cslot, tile_rslot, need_cols, fold_rows, weights, directions):
    n_ex, n_ft = lax.axis_size("ex"), lax.axis_size("ft")
    side = tiles.shape[1]
    col_blocks, num_vecs = directions.shape[0], directions.shape[2]
    row_blocks = weights.shape[0]
    asks, slots = need_cols.shape[2], fold_rows.shape[2]
    ask_rows, slot_rows = num_vecs * asks, num_vecs * slots
    f32, bf16, i32 = jnp.float32, jnp.bfloat16, jnp.int32
    vmem = pl.BlockSpec(memory_space=pltpu.VMEM)
    hbm = pl.BlockSpec(memory_space=pltpu.HBM)
    pairs = [n_ex, n_ft, n_ex, n_ft, n_ex]
    all_slots = n_ft * slot_rows
    width = max(all_slots, 128)
    own = directions.reshape(col_blocks * num_vecs, side)
    out = pl.pallas_call(
        functools.partial(kernel, n_ex, n_ft, num_vecs),
        out_shape=jax.ShapeDtypeStruct((col_blocks * num_vecs, side), f32),
        in_specs=[pl.BlockSpec(memory_space=pltpu.SMEM)] + [hbm] * 7,
        out_specs=vmem,
        scratch_shapes=[
            pltpu.SMEM(tile_cslot.shape, i32),
            pltpu.SMEM(tile_rslot.shape, i32),
            pltpu.SMEM(need_cols.shape, i32),
            pltpu.SMEM((1, slots, n_ft), i32),
            pltpu.VMEM((row_blocks, side), f32),
        ] + [pltpu.SMEM(tile_cslot.shape, i32)] * 4 + [
            pltpu.VMEM(tiles.shape, bf16),
            pltpu.VMEM((col_blocks * num_vecs, side), f32),
            pltpu.VMEM((n_ex, 1, side), i32),
            pltpu.VMEM((n_ex, 1, side), i32),
            pltpu.VMEM((all_slots, width), i32),
            pltpu.VMEM((row_blocks + 8, width), f32),
            pltpu.VMEM((n_ft, row_blocks + 8, width), f32),
            pltpu.VMEM((n_ex, ask_rows, side), bf16),
            pltpu.VMEM((n_ex, ask_rows, side), bf16),
            pltpu.VMEM((all_slots, side), bf16),
            pltpu.VMEM((n_ft, all_slots, side), bf16),
            pltpu.VMEM((n_ex, ask_rows, side), f32),
            pltpu.VMEM((n_ex, ask_rows, side), f32),
            pltpu.VMEM((n_ex * ask_rows, side), f32),
            pltpu.VMEM((n_ft * slot_rows, side), f32),
            pltpu.VMEM((col_blocks * num_vecs, n_ex * ask_rows), bf16),
            pltpu.VMEM((all_slots, n_ft * all_slots), bf16),
            pltpu.VMEM((all_slots, side), f32),
            pltpu.SemaphoreType.DMA((7,)),
        ] + [pltpu.SemaphoreType.DMA((n,)) for n in pairs for _ in range(2)],
        compiler_params=pltpu.CompilerParams(collective_id=0, has_side_effects=True, vmem_limit_bytes=24 << 20),
    )(tile_count, *(pltpu.with_memory_space_constraint(x, pltpu.HBM) for x in (
        tile_cslot, tile_rslot, need_cols, fold_rows.transpose(0, 2, 1),
        weights.reshape(row_blocks, side), tiles, own,
    )))
    return (own + scale_back * out).reshape(directions.shape)


def solution(mesh):
    return jax.shard_map(
        local,
        mesh=mesh,
        in_specs=(
            P(("ex", "ft"), None, None),
            P(("ex", "ft")),
            P(("ex", "ft")),
            P(("ex", "ft")),
            P(("ex", "ft"), None, None),
            P(("ex", "ft"), None, None),
            P("ft", "ex", None),
            P("ex", "ft", None, None),
        ),
        out_specs=P("ex", "ft", None, None),
        check_vma=False,
    )
```
